32 devices in a mesh: rep: 2 (over x), exp: 16 (over z, y, core).
Axes of the slice: x: 2, y: 2, z: 4, core: 2. Of those that a mesh axis runs over, the one named last changes fastest.
Arguments:
- tokens: bfloat16 [1, 128, 7168], P(None, 'exp', 'rep'), may hold values from -6 to 6
- gate_up: bfloat16 [16, 7168, 2, 2048], P('exp', 'rep'), may hold values from -0.09375 to 0.09375
- w_down: bfloat16 [16, 2048, 7168], P('exp', None, 'rep'), may hold values from -0.125 to 0.125
- routes: int32 [1, 128, 8], P(None, 'exp'), may hold values from 0 to 15, all different within a row; in each aligned block of 8 rows (0 to 7, 8 to 15, ..., all dimensions but the last counted through in order) at most 8 rows name the same one
- gates: float32 [1, 128, 8], P(None, 'exp'), may hold values from 0.05 to 1
Outputs:
- mixed_out: bfloat16 [1, 128, 7168], P(None, 'exp', 'rep')
The draws below stay inside these ranges and needn't reach their ends.
Inputs may be any that keep to these rules, and one draw needn't show every extreme that they name: `routes`: within one step, the 8 tokens of one index of exp name any expert at most 8 times, a bound that some block reaches.
All inputs are finite; a program needn't handle non-finite values.
Results may differ from the reference program's by a relative error of at most 0.024.
Values may be sent and summed in bfloat16 or wider, within the bound.
A program may use at most 192 MiB of HBM per device.

```python
import math
import jax
import jax.numpy as jnp
import numpy as np
from jax import lax

D = 7168
FF = 2048
TOP = 8
TOK_DEV = 8
STEPS = 1
EXPERTS = 16
TOKENS = 128
CAP = 8
N_REP = 2
N_EXP = 16


def raised(array, own_key, source, target, parts, factor):
    owner, partner = [(jnp.arange(array.shape[dim]) // (array.shape[dim] // parts)).reshape([-1 if axis == dim else 1 for axis in range(array.ndim)]) for dim in (source, target)]
    chosen = jax.random.permutation(own_key, parts)[partner]
    strong = (owner == chosen) | (owner == (partner + parts // 2) % parts)
    return jnp.where(strong, factor * array, array)


def levels(key, shape, pieces, low, high):
    gain, own = 1.0, jax.random.fold_in(key, 6)
    for axis_at, shards_of in pieces:
        draws = jnp.exp(jax.random.uniform(jax.random.fold_in(own, axis_at), (shards_of,), jnp.float32, low / len(pieces), high / len(pieces)))
        gain = gain * jnp.repeat(draws, shape[axis_at] // shards_of).reshape([-1 if axis == axis_at else 1 for axis in range(len(shape))])
    return gain


def shared_out(key, own, number, rows, amount, top, limit, lean):
    order = jax.random.permutation(key, amount)
    heavy_load, common = portions_of(amount, rows * top, limit, lean, True), portions_of(amount, rows * top, limit, lean, False)
    places = jnp.arange(amount)

    def named(lengths, rotation):
        used = int((lengths > 0).sum())
        fixed = max(1, used // 4)
        shifted = fixed + (places - fixed + rotation * (used - fixed)) % max(1, amount - fixed)
        return jnp.zeros((amount,), jnp.int32).at[order[jnp.where(places < fixed, places, shifted)]].set(jnp.asarray(lengths, jnp.int32))

    lengths = jnp.where(number % 4 == 0, named(heavy_load, number // 4), named(common, number - number // 4 - 1))
    mixed = jax.random.permutation(jax.random.fold_in(own, 3), amount)
    source_of, taker = mixed[0:amount // 2 * 2:2], mixed[1:amount // 2 * 2:2]
    slack = jnp.minimum(lengths[source_of] - 1, limit - lengths[taker]) // 2
    slack = jnp.where((source_of == order[0]) | (taker == order[0]) | (lengths[taker] == 0), 0, jnp.maximum(slack, 0))
    shifted = jax.random.randint(jax.random.fold_in(own, 4), (amount // 2,), 0, 1 << 20) % (slack + 1)
    lengths = lengths.at[source_of].add(-shifted).at[taker].add(shifted)
    items = jnp.searchsorted(jnp.cumsum(lengths), jnp.arange(rows * top), side="right").astype(jnp.int32)
    table = items.reshape(top, rows).T
    table = table[jax.random.permutation(jax.random.fold_in(own, 1), rows)]
    rotation = jax.random.randint(jax.random.fold_in(own, 2), (rows, 1), 0, top)
    return jnp.take_along_axis(table, (jnp.arange(top)[None, :] + rotation) % top, axis=1)


def portions_of(amount, total, limit, slope, full):
    loads = [(1 << 20) // math.isqrt(rank ** slope) + 1 for rank in range(1, amount + 1)]
    largest = limit if full else min(limit, max(-(-total // amount), total * loads[0] // sum(loads)))
    least = 1 if total - largest >= amount - 1 else 0
    counts, surplus = [largest] + [least] * (amount - 1), total - largest - least * (amount - 1)
    while surplus > 0:
        movable = [i for i in range(1, amount) if counts[i] < largest] or [i for i in range(1, amount) if counts[i] < limit]
        mass, remaining = sum([loads[i] for i in movable]), surplus
        for i in movable:
            addition = min(limit - counts[i], max(1, remaining * loads[i] // mass), surplus)
            counts[i] = counts[i] + addition
            surplus = surplus - addition
    return np.array(counts)


def normal_values(rng, dims, spread, limit, split=(), kind=jnp.bfloat16):
    drawn = jax.random.normal(rng, dims, jnp.float32) * spread
    if len(split) > 0:
        drawn = levels(rng, dims, split, -0.22, 0.18) * drawn
    return jnp.clip(drawn, min=-limit, max=limit).astype(kind)


def heavy_noise(own_key, dims, width, bound, cuts, heavy, kind=jnp.bfloat16):
    result = width * jax.random.normal(own_key, dims, jnp.float32)
    if cuts:
        result = result * levels(own_key, dims, cuts, -0.22, 0.18)
    return jnp.clip(raised(result, jax.random.fold_in(own_key, 3), *heavy), -bound, bound).astype(kind)


def setup_inputs(seed: int = 0) -> dict:
    key_list = jax.random.split(jax.random.key(seed), 6)
    tokens = normal_values(key_list[0], (STEPS, TOKENS, D), 1.0, 6.0, ((1, 16), (2, 2)))
    gate_up = heavy_noise(key_list[1], (EXPERTS, D, 2, FF), D ** -0.5, 0.09375, ((0, 16), (1, 2)), (1, 3, 2, 2.0))
    w_down = normal_values(key_list[2], (EXPERTS, FF, D), FF ** -0.5, 0.125, ((0, 16), (2, 2)))
    routes_keys = jax.random.split(jax.random.fold_in(key_list[3], 1), STEPS * TOKENS // TOK_DEV)
    routes_turns = jax.random.permutation(jax.random.fold_in(key_list[3], 3), STEPS * TOKENS // TOK_DEV)
    routes = jax.vmap(lambda own, number: shared_out(jax.random.fold_in(key_list[3], 2), own, number, TOK_DEV, EXPERTS, TOP, CAP, 2))(routes_keys, routes_turns).reshape((STEPS, TOKENS, TOP))
    gates = jnp.clip(jnp.exp(math.log(1.0) - 2.9957323 * jax.random.uniform(key_list[4], (STEPS, TOKENS, TOP), jnp.float32) ** levels(key_list[4], (STEPS, TOKENS, TOP), ((1, 16),), -0.2, 0.2)), 0.05, 1.0)
    return dict(tokens=tokens, gate_up=gate_up, w_down=w_down, routes=routes, gates=gates)


def reference(tokens, gate_up, w_down, routes, gates):
    steps_all, tokens_all, model_width = tokens.shape
    top_count = routes.shape[2]
    experts = gate_up.shape[0]
    hidden_units = w_down.shape[1]
    slab_width = model_width // N_REP
    row_count = N_EXP * CAP
    weights_in = gate_up.reshape(experts, N_REP, slab_width, 2 * hidden_units)

    def one_step(step_index):
        expert_ids = routes[step_index]
        features = tokens[step_index]
        onehot = (expert_ids[:, :, None] == jnp.arange(experts, dtype=jnp.int32)).astype(jnp.int32)
        flat_hot = onehot.reshape(N_EXP, TOK_DEV * top_count, experts)
        before = (jnp.cumsum(flat_hot, axis=1) - flat_hot).astype(jnp.int32)
        slot_rank = jnp.sum(before * flat_hot, axis=2).astype(jnp.int32).reshape(tokens_all, top_count)
        block_index = (jnp.arange(tokens_all, dtype=jnp.int32) // TOK_DEV)[:, None]
        slot_row = (block_index * CAP + slot_rank).astype(jnp.int32)
        token_index = jnp.broadcast_to(jnp.arange(tokens_all, dtype=jnp.int32)[:, None], expert_ids.shape)
        owner_table = jnp.full((experts, row_count), tokens_all, jnp.int32)
        owner_table = owner_table.at[expert_ids.reshape(-1), slot_row.reshape(-1)].set(token_index.reshape(-1))
        padded = jnp.concatenate([features, jnp.zeros((1, model_width), features.dtype)], axis=0)

        def expert_fn(expert_index):
            chosen = padded[owner_table[expert_index]].reshape(row_count, N_REP, slab_width).astype(jnp.float32)
            partials = jnp.einsum("rnf,nfh->nrh", chosen, weights_in[expert_index].astype(jnp.float32))
            partials = lax.optimization_barrier(partials.astype(jnp.bfloat16)).astype(jnp.float32)
            summed = jnp.sum(partials, axis=0)
            gate_part = summed[:, :hidden_units]
            up_part = summed[:, hidden_units:]
            hidden = (jax.nn.silu(gate_part) * up_part).astype(jnp.bfloat16)
            return jnp.dot(hidden, w_down[expert_index], preferred_element_type=jnp.float32).astype(jnp.bfloat16)

        results = lax.map(expert_fn, jnp.arange(experts, dtype=jnp.int32))
        picked = results[expert_ids, slot_row].astype(jnp.float32)
        return jnp.sum(gates[step_index][:, :, None] * picked, axis=1).astype(jnp.bfloat16)

    return jnp.stack([one_step(step_index) for step_index in range(STEPS)])
```

```python
import functools

import jax
import jax.numpy as jnp
from jax import lax
from jax.experimental import pallas as pl
from jax.experimental.pallas import tpu as pltpu
from jax.sharding import PartitionSpec as P


def silu_glu(summed):
    return (jax.nn.silu(summed[:, 0]) * summed[:, 1]).astype(jnp.bfloat16)


def on_device(tokens, gate_up, w_down, routes, gates):
    steps_all, local_tokens, slab_width = tokens.shape
    top_count = routes.shape[2]
    groups = lax.axis_size("exp")
    experts = gate_up.shape[0] * groups
    capacity = max(2, 2 * local_tokens * top_count // experts)
    hidden_units = w_down.shape[1]
    row_count = groups * capacity
    weights_in = gate_up[0].reshape(slab_width, 2 * hidden_units)
    weights_out = w_down[0]
    labels = jnp.arange(experts * capacity, dtype=jnp.int32)
    expert_range = jnp.arange(experts, dtype=jnp.int32)
    expert_ids = routes[0].reshape(-1)
    onehot = (expert_ids[:, None] == expert_range[None, :]).astype(jnp.int32)
    before = jnp.cumsum(onehot, axis=0) - onehot
    slot_rank = jnp.sum(before * onehot, axis=1)
    target_row = expert_ids * capacity + slot_rank
    target_grid = target_row.reshape(local_tokens, top_count)
    placing = jnp.sum(
        (labels[:, None, None] == target_grid[None, :, :]).astype(jnp.int32), axis=2
    ).astype(jnp.bfloat16)
    outgoing = jnp.dot(placing, tokens[0], preferred_element_type=jnp.float32).astype(jnp.bfloat16)
    outgoing = outgoing.reshape(experts, capacity, slab_width)
    arrived = lax.all_to_all(outgoing, "exp", split_axis=0, concat_axis=0, tiled=True)
    partial_value = jnp.dot(
        arrived.reshape(row_count, slab_width), weights_in, preferred_element_type=jnp.float32
    )
    partial_value = partial_value.reshape(row_count, 2, hidden_units)
    shares = lax.psum_scatter(
        partial_value.astype(jnp.bfloat16), "rep", scatter_dimension=0, tiled=True
    ).astype(jnp.float32)
    hidden = silu_glu(shares)
    produced = jnp.dot(
        lax.all_gather(hidden, "rep", axis=0, tiled=True),
        weights_out,
        preferred_element_type=jnp.float32,
    )
    expert_out = produced.astype(jnp.bfloat16).reshape(groups, capacity, slab_width)
    returned = lax.all_to_all(expert_out, "exp", split_axis=0, concat_axis=0, tiled=True).reshape(
        experts * capacity, slab_width
    )
    picked = returned[target_row].reshape(local_tokens, top_count, slab_width).astype(jnp.float32)
    mixed_out = jnp.sum(gates[0][:, :, None] * picked, axis=1).astype(jnp.bfloat16)
    outputs = [mixed_out]
    return jnp.stack(outputs)


def fused_kernel(
    chunks, pieces, lag, tok_ref, gu_ref, dn_ref, routes_ref, gates_ref, out_ref,
    xg, wgu, wdn, x2, pbuf, prec, hid, dacc, cbuf, crec, rbuf, rrec, oacc, fbuf, frec,
    gu_sem, dn_sem, ag_s, ag_r, mi_s, mi_r, dc_s, dc_r,
    ps_s, ps_r, hs_s, hs_r, rc_s, rc_r, rr_s, rr_r, rf_s, rf_r,
):
    rep = lax.axis_index("rep")
    me = lax.axis_index("exp")
    c, y, zl, pair = lax.rem(me, 2), lax.rem(me // 2, 2), lax.rem(me // 4, 2), me // 8
    rows, width = tok_ref.shape
    hidden_units = dn_ref.shape[0]
    n = 16
    cw, pw = hidden_units // chunks, width // pieces
    group, half = 8 * rows, 4 * rows
    other = 1 - rep
    at = zl * 4 + y * 2 + c
    base = pair * 8
    x_peer = (other, me)
    core_peer = (rep, base + zl * 4 + y * 2 + 1 - c)
    far_peer = (rep, (1 - pair) * 8 + at)
    near = [
        (1 - zl, y),
        (1 - zl, 1 - y),
        (zl, 1 - y),
    ]
    near_peers = [(rep, base + a * 4 + b * 2 + c) for a, b in near]

    def remote(src, dst, send, recv, to):
        return pltpu.make_async_remote_copy(
            src_ref=src, dst_ref=dst, send_sem=send, recv_sem=recv,
            device_id=to, device_id_type=pl.DeviceIdType.MESH,
        )

    barrier = pltpu.get_barrier_semaphore()
    peers = [x_peer, core_peer, far_peer] + near_peers
    for peer in peers:
        pl.semaphore_signal(barrier, inc=1, device_id=peer, device_id_type=pl.DeviceIdType.MESH)

    gu_rows = gu_ref.reshape(2 * width, hidden_units)

    def gu_copy(j):
        return pltpu.make_async_copy(
            gu_rows.at[:, pl.ds(pl.multiple_of(j * cw, 128), cw)], wgu.at[j], gu_sem.at[j]
        )

    def dn_copy(q):
        cols = pl.ds(q * pw, pw)
        return pltpu.make_async_copy(dn_ref.at[:, cols], wdn.at[:, cols], dn_sem.at[q])

    for j in range(chunks):
        gu_copy(j).start()
    for q in range(pieces):
        dn_copy(q).start()

    lane = lax.broadcasted_iota(jnp.int32, (rows, 128), 1)
    weight = jnp.zeros((rows, 128), jnp.float32)
    for k in range(routes_ref.shape[1]):
        hit = routes_ref[:, k : k + 1] == lax.rem(lane, n)
        weight = weight + jnp.where(hit, gates_ref[:, k : k + 1], 0.0)
    high = weight.astype(jnp.bfloat16).astype(jnp.float32)
    packed = jnp.where(lane < n, high, jnp.where(lane < 2 * n, weight - high, 0.0))
    xg[0, at, :, 0:width] = tok_ref[...]
    xg[0, at, :, width : width + 128] = packed.astype(jnp.bfloat16)
    pl.semaphore_wait(barrier, len(peers))

    def gather(g, e):
        slot = xg.at[g, at]
        return remote(slot, slot, ag_s.at[g, e], ag_r.at[g, e], near_peers[e])

    def mirror():
        return remote(xg.at[0, at], xg.at[1, at], mi_s, mi_r, far_peer)

    def to_core(g, e):
        a, b = (near + [(zl, y)])[e]
        slot = xg.at[g, a * 4 + b * 2 + c]
        return remote(slot, slot, dc_s.at[g, e], dc_r.at[g, e], core_peer)

    def spread_group(g):
        row_at = lax.broadcasted_iota(jnp.int32, (128, 512), 0)
        col_at = lax.broadcasted_iota(jnp.int32, (128, 512), 1)
        target = jnp.where(col_at < 256, 2 * row_at, 256 + 2 * row_at + 1)
        spread = jnp.where(col_at == target, 1.0, 0.0).astype(jnp.bfloat16)
        batch = 7

        @pl.loop(0, width // (128 * batch))
        def _(t):
            parts = [
                xg[g, :, :, pl.ds(pl.multiple_of((t * batch + i) * 128, 128), 128)].reshape(group, 128)
                for i in range(batch)
            ]
            both = jnp.dot(
                jnp.concatenate(parts, axis=0), spread, preferred_element_type=jnp.float32
            ).astype(jnp.bfloat16)
            for i in range(batch):
                cols = pl.ds(pl.multiple_of((t * batch + i) * 256, 256), 256)
                for h in range(2):
                    r0 = i * group + h * half
                    x2[g, 2 * h * half : (2 * h + 1) * half, cols] = both[r0 : r0 + half, :256]
                    x2[g, (2 * h + 1) * half : (2 * h + 2) * half, cols] = both[r0 : r0 + half, 256:]

    def partial_send(s):
        return remote(pbuf.at[s, other], prec.at[s], ps_s.at[s], ps_r.at[s], x_peer)

    def hidden_send(s):
        return remote(hid.at[s, rep], hid.at[s, rep], hs_s.at[s], hs_r.at[s], x_peer)

    def hidden_recv(s):
        return remote(hid.at[s, other], hid.at[s, other], hs_s.at[s], hs_r.at[s], x_peer)

    def finish(s):
        partial_send(s).wait_recv()
        total = pbuf[s, rep].astype(jnp.float32) + prec[s].astype(jnp.float32)
        hid[s, rep] = (jax.nn.silu(total[:half]) * total[half:]).astype(jnp.bfloat16)
        hidden_send(s).start()

    def up_chunk(g, j):
        acc = jnp.dot(x2[g], wgu[j], preferred_element_type=jnp.float32)
        pbuf[g * chunks + j] = acc.astype(jnp.bfloat16).reshape(2, 2 * half, cw)
        partial_send(g * chunks + j).start()

    for e in range(3):
        gather(0, e).start()
    to_core(0, 3).start()
    mirror().start()
    for e in (2, 0, 1):
        gather(0, e).wait_recv()
        to_core(0, e).start()
    for e in range(4):
        to_core(0, e).wait_recv()
    spread_group(0)
    mirror().wait_recv()
    for e in range(3):
        gather(1, e).start()
    to_core(1, 3).start()

    @pl.loop(0, chunks)
    def _(j):
        gu_copy(j).wait()
        up_chunk(0, j)

        @pl.when(j >= lag)
        def _():
            finish(j - lag)

    early = 2
    for j in range(early):
        finish(chunks - lag + j)
    for e in (2, 0, 1):
        gather(1, e).wait_recv()
        to_core(1, e).start()
    for e in range(4):
        to_core(1, e).wait_recv()
    spread_group(1)

    @pl.loop(0, chunks)
    def _(j):
        up_chunk(1, j)

        @pl.when(j >= early)
        def _():
            finish(chunks + j - lag)

    mark = lax.broadcasted_iota(jnp.int32, (group, 128), 1)

    def scale_of(g):
        lanes = xg[g, :, :, width : width + 128].reshape(group, 128).astype(jnp.float32)
        return jnp.sum(jnp.where(lax.rem(mark, n) == me, lanes, 0.0), axis=1, keepdims=True)

    def hidden_cols(g, j0, j1):
        return jnp.concatenate(
            [hid[g * chunks + j].reshape(group, cw) for j in range(j0, j1)], axis=1
        )

    def core_send(g, q):
        return remote(cbuf.at[g, q, 1 - c], crec.at[g, q], rc_s.at[g, q], rc_r.at[g, q], core_peer)

    def near_send(g, q, e):
        a, b = near[e]
        return remote(
            rbuf.at[g, q, a * 2 + b], rrec.at[g, q, e], rr_s.at[g, q, e], rr_r.at[g, q, e], near_peers[e]
        )

    def far_send(q):
        return remote(fbuf.at[q], frec.at[q], rf_s.at[q], rf_r.at[q], far_peer)

    def hand_out(g, q, made):
        mixed = (made.astype(jnp.bfloat16).astype(jnp.float32) * scale_of(g)).astype(jnp.bfloat16)
        mixed = mixed.reshape(8, rows, pw)
        for b in range(8):
            cbuf[g, q, b % 2, b // 2] = mixed[b]
        core_send(g, q).start()

    def produce(q):
        made = jnp.dot(
            hidden_cols(0, 0, chunks), wdn[:, q * pw : (q + 1) * pw], preferred_element_type=jnp.float32
        )
        hand_out(0, q, made)

    mid = chunks // 2

    def first_part(q):
        dacc[:, q * pw : (q + 1) * pw] = jnp.dot(
            hidden_cols(1, 0, mid), wdn[: mid * cw, q * pw : (q + 1) * pw],
            preferred_element_type=jnp.float32,
        )

    def second_part(q):
        made = dacc[:, q * pw : (q + 1) * pw] + jnp.dot(
            hidden_cols(1, mid, chunks), wdn[mid * cw :, q * pw : (q + 1) * pw],
            preferred_element_type=jnp.float32,
        )
        hand_out(1, q, made)

    def over_core(g, q):
        core_send(g, q).wait_recv()
        rbuf[g, q] = (cbuf[g, q, c].astype(jnp.float32) + crec[g, q].astype(jnp.float32)).astype(jnp.bfloat16)
        for e in range(3):
            near_send(g, q, e).start()

    def over_near(g, q):
        total = rbuf[g, q, zl * 2 + y].astype(jnp.float32)
        for e in range(3):
            near_send(g, q, e).wait_recv()
            total = total + rrec[g, q, e].astype(jnp.float32)
        if g == 0:
            oacc[q] = total
        else:
            fbuf[q] = total.astype(jnp.bfloat16)
            far_send(q).start()

    def last(q):
        far_send(q).wait_recv()
        out_ref[:, q * pw : (q + 1) * pw] = (oacc[q] + frec[q].astype(jnp.float32)).astype(jnp.bfloat16)

    rest = [2 * chunks - lag + i for i in range(lag)]
    for q in range(pieces):
        dn_copy(q).wait()
    for s in range(chunks):
        hidden_recv(s).wait_recv()
    finish(rest.pop(0))
    for q in range(pieces):
        produce(q)
        if rest:
            finish(rest.pop(0))
    for q in range(pieces):
        over_core(0, q)
        if rest:
            finish(rest.pop(0))
    while rest:
        finish(rest.pop(0))
    for s in range(chunks, chunks + mid):
        hidden_recv(s).wait_recv()
    for q in range(pieces):
        first_part(q)
    for q in range(pieces):
        over_near(0, q)
    for s in range(chunks + mid, 2 * chunks):
        hidden_recv(s).wait_recv()
    for step in range(pieces + 3):
        if step < pieces:
            second_part(step)
        if 0 <= step - 1 < pieces:
            over_core(1, step - 1)
        if 0 <= step - 2 < pieces:
            over_near(1, step - 2)
        if 0 <= step - 3 < pieces:
            last(step - 3)

    mirror().wait_send()
    for g in range(2):
        for e in range(3):
            gather(g, e).wait_send()
        for e in range(4):
            to_core(g, e).wait_send()
        for q in range(pieces):
            core_send(g, q).wait_send()
            for e in range(3):
                near_send(g, q, e).wait_send()
    for s in range(2 * chunks):
        partial_send(s).wait_send()
        hidden_send(s).wait_send()
    for q in range(pieces):
        far_send(q).wait_send()


def fused_on_device(tokens, gate_up, w_down, routes, gates):
    _, rows, width = tokens.shape
    hidden_units = w_down.shape[1]
    chunks, pieces, lag = hidden_units // 256, 2, 5
    pw, group, half = width // pieces, 8 * rows, 4 * rows
    bf16, dma = jnp.bfloat16, pltpu.SemaphoreType.DMA
    vmem = pl.BlockSpec(memory_space=pltpu.VMEM)
    anywhere = pl.BlockSpec(memory_space=pl.ANY)
    mixed_out = pl.pallas_call(
        functools.partial(fused_kernel, chunks, pieces, lag),
        out_shape=jax.ShapeDtypeStruct((rows, width), bf16),
        in_specs=[vmem, anywhere, anywhere, vmem, vmem],
        out_specs=vmem,
        scratch_shapes=[
            pltpu.VMEM((2, 8, rows, width + 128), bf16),
            pltpu.VMEM((chunks, 2 * width, 256), bf16),
            pltpu.VMEM((hidden_units, width), bf16),
            pltpu.VMEM((2, 2 * group, 2 * width), bf16),
            pltpu.VMEM((2 * chunks, 2, 2 * half, 256), bf16),
            pltpu.VMEM((2 * chunks, 2 * half, 256), bf16),
            pltpu.VMEM((2 * chunks, 2, half, 256), bf16),
            pltpu.VMEM((group, width), jnp.float32),
            pltpu.VMEM((2, pieces, 2, 4, rows, pw), bf16),
            pltpu.VMEM((2, pieces, 4, rows, pw), bf16),
            pltpu.VMEM((2, pieces, 4, rows, pw), bf16),
            pltpu.VMEM((2, pieces, 3, rows, pw), bf16),
            pltpu.VMEM((pieces, rows, pw), jnp.float32),
            pltpu.VMEM((pieces, rows, pw), bf16),
            pltpu.VMEM((pieces, rows, pw), bf16),
            dma((chunks,)), dma((pieces,)),
            dma((2, 3)), dma((2, 3)), dma(()), dma(()), dma((2, 4)), dma((2, 4)),
            dma((2 * chunks,)), dma((2 * chunks,)), dma((2 * chunks,)), dma((2 * chunks,)),
            dma((2, pieces)), dma((2, pieces)), dma((2, pieces, 3)), dma((2, pieces, 3)),
            dma((pieces,)), dma((pieces,)),
        ],
        compiler_params=pltpu.CompilerParams(
            collective_id=0, has_side_effects=True, vmem_limit_bytes=67043328
        ),
    )(tokens[0], gate_up[0], w_down[0], routes[0], gates[0])
    return mixed_out[None]


def fits(mesh):
    return mesh.shape["rep"] == 2 and mesh.shape["exp"] == 16


def solution(mesh):
    placed = (
        P(None, "exp", "rep"),
        P("exp", "rep", None, None),
        P("exp", None, "rep"),
        P(None, "exp", None),
        P(None, "exp", None),
    )
    return jax.shard_map(
        fused_on_device if fits(mesh) else on_device, mesh=mesh, in_specs=placed, out_specs=P(None, "exp", "rep"), check_vma=False
    )
```

```python
import functools

import jax
import jax.numpy as jnp
from jax import lax
from jax.experimental import pallas as pl
from jax.experimental.pallas import tpu as pltpu
from jax.sharding import PartitionSpec as P


def silu_glu(summed):
    return (jax.nn.silu(summed[:, 0]) * summed[:, 1]).astype(jnp.bfloat16)


def on_device(tokens, gate_up, w_down, routes, gates):
    steps_all, local_tokens, slab_width = tokens.shape
    top_count = routes.shape[2]
    groups = lax.axis_size("exp")
    experts = gate_up.shape[0] * groups
    capacity = max(2, 2 * local_tokens * top_count // experts)
    hidden_units = w_down.shape[1]
    row_count = groups * capacity
    weights_in = gate_up[0].reshape(slab_width, 2 * hidden_units)
    weights_out = w_down[0]
    labels = jnp.arange(experts * capacity, dtype=jnp.int32)
    expert_range = jnp.arange(experts, dtype=jnp.int32)
    expert_ids = routes[0].reshape(-1)
    onehot = (expert_ids[:, None] == expert_range[None, :]).astype(jnp.int32)
    before = jnp.cumsum(onehot, axis=0) - onehot
    slot_rank = jnp.sum(before * onehot, axis=1)
    target_row = expert_ids * capacity + slot_rank
    target_grid = target_row.reshape(local_tokens, top_count)
    placing = jnp.sum(
        (labels[:, None, None] == target_grid[None, :, :]).astype(jnp.int32), axis=2
    ).astype(jnp.bfloat16)
    outgoing = jnp.dot(placing, tokens[0], preferred_element_type=jnp.float32).astype(jnp.bfloat16)
    outgoing = outgoing.reshape(experts, capacity, slab_width)
    arrived = lax.all_to_all(outgoing, "exp", split_axis=0, concat_axis=0, tiled=True)
    partial_value = jnp.dot(
        arrived.reshape(row_count, slab_width), weights_in, preferred_element_type=jnp.float32
    )
    partial_value = partial_value.reshape(row_count, 2, hidden_units)
    shares = lax.psum_scatter(
        partial_value.astype(jnp.bfloat16), "rep", scatter_dimension=0, tiled=True
    ).astype(jnp.float32)
    hidden = silu_glu(shares)
    produced = jnp.dot(
        lax.all_gather(hidden, "rep", axis=0, tiled=True),
        weights_out,
        preferred_element_type=jnp.float32,
    )
    expert_out = produced.astype(jnp.bfloat16).reshape(groups, capacity, slab_width)
    returned = lax.all_to_all(expert_out, "exp", split_axis=0, concat_axis=0, tiled=True).reshape(
        experts * capacity, slab_width
    )
    picked = returned[target_row].reshape(local_tokens, top_count, slab_width).astype(jnp.float32)
    mixed_out = jnp.sum(gates[0][:, :, None] * picked, axis=1).astype(jnp.bfloat16)
    outputs = [mixed_out]
    return jnp.stack(outputs)


def fused_kernel(
    chunks, pieces, tok_ref, gu_ref, dn_ref, routes_ref, gates_ref, out_ref,
    xg, wgu, wdn, x2, pbuf, prec, hid, dacc, cbuf, crec, rbuf, rrec, oacc, fbuf, frec,
    picks, shares, obuf, in_sem, out_sem, gu_sem, dn_sem, ag_s, ag_r, mi_s, mi_r, dc_s, dc_r,
    ps_s, ps_r, hs_s, hs_r, rc_s, rc_r, rr_s, rr_r, rf_s, rf_r,
):
    rep = lax.axis_index("rep")
    me = lax.axis_index("exp")
    c, y, zl, pair = lax.rem(me, 2), lax.rem(me // 2, 2), lax.rem(me // 4, 2), me // 8
    rows, width = tok_ref.shape
    hidden_units = dn_ref.shape[0]
    n = 16
    cw, pw = hidden_units // chunks, width // pieces
    group, half = 8 * rows, 4 * rows
    other = 1 - rep
    at = zl * 4 + y * 2 + c
    base = pair * 8
    x_peer = (other, me)
    core_peer = (rep, base + zl * 4 + y * 2 + 1 - c)
    far_peer = (rep, (1 - pair) * 8 + at)
    near = [
        (1 - zl, y),
        (1 - zl, 1 - y),
        (zl, 1 - y),
    ]
    near_peers = [(rep, base + a * 4 + b * 2 + c) for a, b in near]

    def remote(src, dst, send, recv, to):
        return pltpu.make_async_remote_copy(
            src_ref=src, dst_ref=dst, send_sem=send, recv_sem=recv,
            device_id=to, device_id_type=pl.DeviceIdType.MESH,
        )

    barrier = pltpu.get_barrier_semaphore()
    peers = [x_peer, core_peer, far_peer] + near_peers
    for peer in peers:
        pl.semaphore_signal(barrier, inc=1, device_id=peer, device_id_type=pl.DeviceIdType.MESH)

    gu_rows = gu_ref.reshape(2 * width, hidden_units)

    def gu_copy(j):
        return pltpu.make_async_copy(
            gu_rows.at[:, pl.ds(pl.multiple_of(j * cw, 128), cw)], wgu.at[j], gu_sem.at[j]
        )

    mid = chunks // 2

    def dn_copy(k):
        part = pl.ds(k * mid * cw, mid * cw)
        return pltpu.make_async_copy(dn_ref.at[part], wdn.at[part], dn_sem.at[k])

    own = [
        pltpu.make_async_copy(routes_ref, picks, in_sem.at[0]),
        pltpu.make_async_copy(gates_ref, shares, in_sem.at[1]),
        pltpu.make_async_copy(tok_ref, xg.at[0, at, :, pl.ds(0, width)], in_sem.at[2]),
    ]
    for copy in own:
        copy.start()
    for j in range(chunks):
        gu_copy(j).start()
    own[0].wait()
    own[1].wait()
    lane = lax.broadcasted_iota(jnp.int32, (rows, 128), 1)
    weight = jnp.zeros((rows, 128), jnp.float32)
    for k in range(picks.shape[1]):
        hit = picks[:, k : k + 1] == lax.rem(lane, n)
        weight = weight + jnp.where(hit, shares[:, k : k + 1], 0.0)
    high = weight.astype(jnp.bfloat16).astype(jnp.float32)
    packed = jnp.where(lane < n, high, jnp.where(lane < 2 * n, weight - high, 0.0))
    xg[0, at, :, width : width + 128] = packed.astype(jnp.bfloat16)
    own[2].wait()
    pl.semaphore_wait(barrier, len(peers))

    def gather(g, e):
        slot = xg.at[g, at]
        return remote(slot, slot, ag_s.at[g, e], ag_r.at[g, e], near_peers[e])

    def mirror():
        return remote(xg.at[0, at], xg.at[1, at], mi_s, mi_r, far_peer)

    def to_core(g, e):
        a, b = (near + [(zl, y)])[e]
        slot = xg.at[g, a * 4 + b * 2 + c]
        return remote(slot, slot, dc_s.at[g, e], dc_r.at[g, e], core_peer)

    def spread_group(g):
        row_at = lax.broadcasted_iota(jnp.int32, (128, 512), 0)
        col_at = lax.broadcasted_iota(jnp.int32, (128, 512), 1)
        target = jnp.where(col_at < 256, 2 * row_at, 256 + 2 * row_at + 1)
        spread = jnp.where(col_at == target, 1.0, 0.0).astype(jnp.bfloat16)
        batch = 7

        @pl.loop(0, width // (128 * batch))
        def _(t):
            parts = [
                xg[g, :, :, pl.ds(pl.multiple_of((t * batch + i) * 128, 128), 128)].reshape(group, 128)
                for i in range(batch)
            ]
            both = jnp.dot(
                jnp.concatenate(parts, axis=0), spread, preferred_element_type=jnp.float32
            ).astype(jnp.bfloat16)
            for i in range(batch):
                cols = pl.ds(pl.multiple_of((t * batch + i) * 256, 256), 256)
                for h in range(2):
                    r0 = i * group + h * half
                    x2[g, 2 * h * half : (2 * h + 1) * half, cols] = both[r0 : r0 + half, :256]
                    x2[g, (2 * h + 1) * half : (2 * h + 2) * half, cols] = both[r0 : r0 + half, 256:]

    def partial_send(s):
        return remote(pbuf.at[s, other], prec.at[s], ps_s.at[s], ps_r.at[s], x_peer)

    def hidden_send(s):
        return remote(hid.at[s, rep], hid.at[s, rep], hs_s.at[s], hs_r.at[s], x_peer)

    def hidden_recv(s):
        return remote(hid.at[s, other], hid.at[s, other], hs_s.at[s], hs_r.at[s], x_peer)

    def finish(s):
        partial_send(s).wait_recv()
        total = pbuf[s, rep].astype(jnp.float32) + prec[s].astype(jnp.float32)
        hid[s, rep] = (jax.nn.silu(total[:half]) * total[half:]).astype(jnp.bfloat16)
        hidden_send(s).start()

    def up_chunk(g, j):
        acc = jnp.dot(x2[g], wgu[j], preferred_element_type=jnp.float32)
        pbuf[g * chunks + j] = acc.astype(jnp.bfloat16).reshape(2, 2 * half, cw)
        partial_send(g * chunks + j).start()

    for e in range(3):
        gather(0, e).start()
    to_core(0, 3).start()
    mirror().start()
    for e in (2, 0, 1):
        gather(0, e).wait_recv()
        to_core(0, e).start()
    for e in range(4):
        to_core(0, e).wait_recv()
    for k in range(2):
        dn_copy(k).start()
    spread_group(0)
    mirror().wait_recv()
    for e in range(3):
        gather(1, e).start()
    to_core(1, 3).start()

    @pl.loop(0, chunks)
    def _(j):
        gu_copy(j).wait()
        up_chunk(0, j)

    early = 2
    for j in range(early):
        finish(j)
    for e in (2, 0, 1):
        gather(1, e).wait_recv()
        to_core(1, e).start()
    for e in range(4):
        to_core(1, e).wait_recv()
    spread_group(1)
    lag = 5

    @pl.loop(0, chunks)
    def _(j):
        up_chunk(1, j)

        @pl.when(j < mid - early)
        def _():
            finish(early + j)

        @pl.when(j >= lag)
        def _():
            finish(chunks + j - lag)

    mark = lax.broadcasted_iota(jnp.int32, (group, 128), 1)

    def scale_of(g):
        lanes = xg[g, :, :, width : width + 128].reshape(group, 128).astype(jnp.float32)
        return jnp.sum(jnp.where(lax.rem(mark, n) == me, lanes, 0.0), axis=1, keepdims=True)

    scales = [scale_of(g) for g in range(2)]

    def hidden_cols(g, j0, j1):
        return jnp.concatenate(
            [hid[g * chunks + j].reshape(group, cw) for j in range(j0, j1)], axis=1
        )

    def core_send(g, q):
        return remote(cbuf.at[g, q, 1 - c], crec.at[g, q], rc_s.at[g, q], rc_r.at[g, q], core_peer)

    def near_send(g, q, e):
        a, b = near[e]
        return remote(
            rbuf.at[g, q, a * 2 + b], rrec.at[g, q, e], rr_s.at[g, q, e], rr_r.at[g, q, e], near_peers[e]
        )

    def far_send(q):
        return remote(fbuf.at[q], frec.at[q], rf_s.at[q], rf_r.at[q], far_peer)

    def hand_out(g, q, made):
        mixed = (made.astype(jnp.bfloat16).astype(jnp.float32) * scales[g]).astype(jnp.bfloat16)
        mixed = mixed.reshape(8, rows, pw)
        for b in range(8):
            cbuf[g, q, b % 2, b // 2] = mixed[b]
        core_send(g, q).start()

    def first_part(g, q):
        cols = slice(q * pw, (q + 1) * pw)
        dacc[g, :, cols] = jnp.dot(
            hidden_cols(g, 0, mid), wdn[: mid * cw, cols], preferred_element_type=jnp.float32
        )

    def second_part(g, q):
        cols = slice(q * pw, (q + 1) * pw)
        made = dacc[g, :, cols] + jnp.dot(
            hidden_cols(g, mid, chunks), wdn[mid * cw :, cols], preferred_element_type=jnp.float32
        )
        hand_out(g, q, made)

    def over_core(g, q):
        core_send(g, q).wait_recv()
        rbuf[g, q] = (cbuf[g, q, c].astype(jnp.float32) + crec[g, q].astype(jnp.float32)).astype(jnp.bfloat16)
        for e in range(3):
            near_send(g, q, e).start()

    def over_near(g, q):
        total = rbuf[g, q, zl * 2 + y].astype(jnp.float32)
        for e in range(3):
            near_send(g, q, e).wait_recv()
            total = total + rrec[g, q, e].astype(jnp.float32)
        if g == 0:
            oacc[q] = total
        else:
            fbuf[q] = total.astype(jnp.bfloat16)
            far_send(q).start()

    def put(q):
        cols = pl.ds(q * pw, pw)
        return pltpu.make_async_copy(obuf.at[:, cols], out_ref.at[:, cols], out_sem.at[q])

    def last(q):
        far_send(q).wait_recv()
        obuf[:, q * pw : (q + 1) * pw] = (oacc[q] + frec[q].astype(jnp.float32)).astype(jnp.bfloat16)
        put(q).start()

    for k in range(2):
        dn_copy(k).wait()
    for s in range(mid):
        hidden_recv(s).wait_recv()
    late = [2 * chunks - lag + i for i in range(lag)]
    spare = list(range(mid, chunks))
    for q in range(pieces):
        first_part(0, q)
        if q % 2 == 1 and late:
            finish(late.pop(0))
            if spare:
                finish(spare.pop(0))
    while late:
        if spare:
            finish(spare.pop(0))
        finish(late.pop(0))
    while spare:
        finish(spare.pop(0))
    for s in range(chunks, chunks + mid):
        hidden_recv(s).wait_recv()
    for q in range(pieces):
        first_part(1, q)
    for s in range(chunks + mid, 2 * chunks):
        hidden_recv(s).wait_recv()
    behind = 4
    for q in range(pieces):
        second_part(1, q)
        if q >= behind:
            over_core(1, q - behind)
    for s in range(mid, chunks):
        hidden_recv(s).wait_recv()
    for q in range(pieces):
        second_part(0, q)
        if pieces - behind + q < pieces:
            over_core(1, pieces - behind + q)
        if q >= behind:
            over_core(0, q - behind)
    for q in range(pieces - behind, pieces):
        over_core(0, q)
    for q in range(pieces):
        over_near(1, q)
    for q in range(pieces):
        over_near(0, q)
    for q in range(pieces):
        last(q)

    mirror().wait_send()
    for g in range(2):
        for e in range(3):
            gather(g, e).wait_send()
        for e in range(4):
            to_core(g, e).wait_send()
        for q in range(pieces):
            core_send(g, q).wait_send()
            for e in range(3):
                near_send(g, q, e).wait_send()
    for s in range(2 * chunks):
        partial_send(s).wait_send()
        hidden_send(s).wait_send()
    for q in range(pieces):
        far_send(q).wait_send()
        put(q).wait()


def fused_on_device(tokens, gate_up, w_down, routes, gates):
    _, rows, width = tokens.shape
    hidden_units = w_down.shape[1]
    chunks, pieces = hidden_units // 256, width // 512
    pw, group, half = width // pieces, 8 * rows, 4 * rows
    bf16, dma = jnp.bfloat16, pltpu.SemaphoreType.DMA
    anywhere = pl.BlockSpec(memory_space=pl.ANY)
    mixed_out = pl.pallas_call(
        functools.partial(fused_kernel, chunks, pieces),
        out_shape=jax.ShapeDtypeStruct((rows, width), bf16),
        in_specs=[anywhere] * 5,
        out_specs=anywhere,
        scratch_shapes=[
            pltpu.VMEM((2, 8, rows, width + 128), bf16),
            pltpu.VMEM((chunks, 2 * width, 256), bf16),
            pltpu.VMEM((hidden_units, width), bf16),
            pltpu.VMEM((2, 2 * group, 2 * width), bf16),
            pltpu.VMEM((2 * chunks, 2, 2 * half, 256), bf16),
            pltpu.VMEM((2 * chunks, 2 * half, 256), bf16),
            pltpu.VMEM((2 * chunks, 2, half, 256), bf16),
            pltpu.VMEM((2, group, width), jnp.float32),
            pltpu.VMEM((2, pieces, 2, 4, rows, pw), bf16),
            pltpu.VMEM((2, pieces, 4, rows, pw), bf16),
            pltpu.VMEM((2, pieces, 4, rows, pw), bf16),
            pltpu.VMEM((2, pieces, 3, rows, pw), bf16),
            pltpu.VMEM((pieces, rows, pw), jnp.float32),
            pltpu.VMEM((pieces, rows, pw), bf16),
            pltpu.VMEM((pieces, rows, pw), bf16),
            pltpu.VMEM(routes.shape[1:], routes.dtype),
            pltpu.VMEM(gates.shape[1:], gates.dtype),
            pltpu.VMEM((rows, width), bf16),
            dma((3,)), dma((pieces,)), dma((chunks,)), dma((2,)),
            dma((2, 3)), dma((2, 3)), dma(()), dma(()), dma((2, 4)), dma((2, 4)),
            dma((2 * chunks,)), dma((2 * chunks,)), dma((2 * chunks,)), dma((2 * chunks,)),
            dma((2, pieces)), dma((2, pieces)), dma((2, pieces, 3)), dma((2, pieces, 3)),
            dma((pieces,)), dma((pieces,)),
        ],
        compiler_params=pltpu.CompilerParams(
            collective_id=0, has_side_effects=True, vmem_limit_bytes=67043328
        ),
    )(tokens[0], gate_up[0], w_down[0], routes[0], gates[0])
    return mixed_out[None]


def fits(mesh):
    return mesh.shape["rep"] == 2 and mesh.shape["exp"] == 16


def solution(mesh):
    placed = (
        P(None, "exp", "rep"),
        P("exp", "rep", None, None),
        P("exp", None, "rep"),
        P(None, "exp", None),
        P(None, "exp", None),
    )
    return jax.shard_map(
        fused_on_device if fits(mesh) else on_device, mesh=mesh, in_specs=placed, out_specs=P(None, "exp", "rep"), check_vma=False
    )
```

```python
import functools

import jax
import jax.numpy as jnp
from jax import lax
from jax.experimental import pallas as pl
from jax.experimental.pallas import tpu as pltpu
from jax.sharding import PartitionSpec as P


def silu_glu(summed):
    return (jax.nn.silu(summed[:, 0]) * summed[:, 1]).astype(jnp.bfloat16)


def on_device(tokens, gate_up, w_down, routes, gates):
    steps_all, local_tokens, slab_width = tokens.shape
    top_count = routes.shape[2]
    groups = lax.axis_size("exp")
    experts = gate_up.shape[0] * groups
    capacity = max(2, 2 * local_tokens * top_count // experts)
    hidden_units = w_down.shape[1]
    row_count = groups * capacity
    weights_in = gate_up[0].reshape(slab_width, 2 * hidden_units)
    weights_out = w_down[0]
    labels = jnp.arange(experts * capacity, dtype=jnp.int32)
    expert_range = jnp.arange(experts, dtype=jnp.int32)
    expert_ids = routes[0].reshape(-1)
    onehot = (expert_ids[:, None] == expert_range[None, :]).astype(jnp.int32)
    before = jnp.cumsum(onehot, axis=0) - onehot
    slot_rank = jnp.sum(before * onehot, axis=1)
    target_row = expert_ids * capacity + slot_rank
    target_grid = target_row.reshape(local_tokens, top_count)
    placing = jnp.sum(
        (labels[:, None, None] == target_grid[None, :, :]).astype(jnp.int32), axis=2
    ).astype(jnp.bfloat16)
    outgoing = jnp.dot(placing, tokens[0], preferred_element_type=jnp.float32).astype(jnp.bfloat16)
    outgoing = outgoing.reshape(experts, capacity, slab_width)
    arrived = lax.all_to_all(outgoing, "exp", split_axis=0, concat_axis=0, tiled=True)
    partial_value = jnp.dot(
        arrived.reshape(row_count, slab_width), weights_in, preferred_element_type=jnp.float32
    )
    partial_value = partial_value.reshape(row_count, 2, hidden_units)
    shares = lax.psum_scatter(
        partial_value.astype(jnp.bfloat16), "rep", scatter_dimension=0, tiled=True
    ).astype(jnp.float32)
    hidden = silu_glu(shares)
    produced = jnp.dot(
        lax.all_gather(hidden, "rep", axis=0, tiled=True),
        weights_out,
        preferred_element_type=jnp.float32,
    )
    expert_out = produced.astype(jnp.bfloat16).reshape(groups, capacity, slab_width)
    returned = lax.all_to_all(expert_out, "exp", split_axis=0, concat_axis=0, tiled=True).reshape(
        experts * capacity, slab_width
    )
    picked = returned[target_row].reshape(local_tokens, top_count, slab_width).astype(jnp.float32)
    mixed_out = jnp.sum(gates[0][:, :, None] * picked, axis=1).astype(jnp.bfloat16)
    outputs = [mixed_out]
    return jnp.stack(outputs)


def fused_kernel(
    chunks, pieces, tok_ref, gu_ref, dn_ref, routes_ref, gates_ref, near_ref, far_ref,
    xg, wgu, wdn, x2, pbuf, prec, hid, dacc, cbuf, crec, rbuf, rrec, oacc, fbuf,
    picks, shares, in_sem, out_sem, gu_sem, dn_sem, ag_s, ag_r, mi_s, mi_r, dc_s, dc_r,
    ps_s, ps_r, hs_s, hs_r, rc_s, rc_r, rr_s, rr_r, rf_s, rf_r,
):
    rep = lax.axis_index("rep")
    me = lax.axis_index("exp")
    c, y, zl, pair = lax.rem(me, 2), lax.rem(me // 2, 2), lax.rem(me // 4, 2), me // 8
    rows, width = tok_ref.shape
    hidden_units = dn_ref.shape[0]
    n = 16
    cw, pw = hidden_units // chunks, width // pieces
    group, half = 8 * rows, 4 * rows
    other = 1 - rep
    at = zl * 4 + y * 2 + c
    base = pair * 8
    x_peer = (other, me)
    core_peer = (rep, base + zl * 4 + y * 2 + 1 - c)
    far_peer = (rep, (1 - pair) * 8 + at)
    near = [
        (1 - zl, y),
        (1 - zl, 1 - y),
        (zl, 1 - y),
    ]
    near_peers = [(rep, base + a * 4 + b * 2 + c) for a, b in near]

    def remote(src, dst, send, recv, to):
        return pltpu.make_async_remote_copy(
            src_ref=src, dst_ref=dst, send_sem=send, recv_sem=recv,
            device_id=to, device_id_type=pl.DeviceIdType.MESH,
        )

    barrier = pltpu.get_barrier_semaphore()
    peers = [x_peer, core_peer, far_peer] + near_peers
    for peer in peers:
        pl.semaphore_signal(barrier, inc=1, device_id=peer, device_id_type=pl.DeviceIdType.MESH)

    gu_rows = gu_ref.reshape(2 * width, hidden_units)

    def gu_copy(j):
        return pltpu.make_async_copy(
            gu_rows.at[:, pl.ds(pl.multiple_of(j * cw, 128), cw)], wgu.at[j], gu_sem.at[j]
        )

    mid = chunks // 2

    def dn_copy(k):
        part = pl.ds(k * mid * cw, mid * cw)
        return pltpu.make_async_copy(dn_ref.at[part], wdn.at[part], dn_sem.at[k])

    own = [
        pltpu.make_async_copy(routes_ref, picks, in_sem.at[0]),
        pltpu.make_async_copy(gates_ref, shares, in_sem.at[1]),
        pltpu.make_async_copy(tok_ref, xg.at[0, at, :, pl.ds(0, width)], in_sem.at[2]),
    ]
    for copy in own:
        copy.start()
    for j in range(chunks):
        gu_copy(j).start()
    own[0].wait()
    own[1].wait()
    lane = lax.broadcasted_iota(jnp.int32, (rows, 128), 1)
    weight = jnp.zeros((rows, 128), jnp.float32)
    for k in range(picks.shape[1]):
        hit = picks[:, k : k + 1] == lax.rem(lane, n)
        weight = weight + jnp.where(hit, shares[:, k : k + 1], 0.0)
    high = weight.astype(jnp.bfloat16).astype(jnp.float32)
    packed = jnp.where(lane < n, high, jnp.where(lane < 2 * n, weight - high, 0.0))
    xg[0, at, :, width : width + 128] = packed.astype(jnp.bfloat16)
    own[2].wait()
    pl.semaphore_wait(barrier, len(peers))

    def gather(g, e):
        slot = xg.at[g, at]
        return remote(slot, slot, ag_s.at[g, e], ag_r.at[g, e], near_peers[e])

    def mirror():
        return remote(xg.at[0, at], xg.at[1, at], mi_s, mi_r, far_peer)

    def to_core(g, e):
        a, b = (near + [(zl, y)])[e]
        slot = xg.at[g, a * 4 + b * 2 + c]
        return remote(slot, slot, dc_s.at[g, e], dc_r.at[g, e], core_peer)

    def spread_half(g, h):
        row_at = lax.broadcasted_iota(jnp.int32, (128, 512), 0)
        col_at = lax.broadcasted_iota(jnp.int32, (128, 512), 1)
        target = jnp.where(col_at < 256, 2 * row_at, 256 + 2 * row_at + 1)
        spread = jnp.where(col_at == target, 1.0, 0.0).astype(jnp.bfloat16)
        batch = 14

        @pl.loop(0, width // (128 * batch))
        def _(t):
            parts = [
                xg[g, pl.ds(h * 4, 4), :, pl.ds(pl.multiple_of((t * batch + i) * 128, 128), 128)].reshape(half, 128)
                for i in range(batch)
            ]
            both = jnp.dot(
                jnp.concatenate(parts, axis=0), spread, preferred_element_type=jnp.float32
            ).astype(jnp.bfloat16)
            for i in range(batch):
                cols = pl.ds(pl.multiple_of((t * batch + i) * 256, 256), 256)
                x2[g, h, :half, cols] = both[i * half : (i + 1) * half, :256]
                x2[g, h, half:, cols] = both[i * half : (i + 1) * half, 256:]

    def partial_send(s):
        return remote(pbuf.at[s, other], prec.at[s], ps_s.at[s], ps_r.at[s], x_peer)

    def hidden_send(s):
        return remote(hid.at[s, rep], hid.at[s, rep], hs_s.at[s], hs_r.at[s], x_peer)

    def hidden_recv(s):
        return remote(hid.at[s, other], hid.at[s, other], hs_s.at[s], hs_r.at[s], x_peer)

    def finish(s):
        partial_send(s).wait_recv()
        total = pbuf[s, rep].astype(jnp.float32) + prec[s].astype(jnp.float32)
        hid[s, rep] = (jax.nn.silu(total[:half]) * total[half:]).astype(jnp.bfloat16)
        hidden_send(s).start()

    def up_chunk(g, j):
        acc = jnp.dot(x2[g].reshape(2 * group, 2 * width), wgu[j], preferred_element_type=jnp.float32)
        pbuf[g * chunks + j] = acc.astype(jnp.bfloat16).reshape(2, 2 * half, cw)
        partial_send(g * chunks + j).start()

    for e in range(3):
        gather(0, e).start()
    to_core(0, 3).start()
    mirror().start()
    for e in (2, 0):
        gather(0, e).wait_recv()
        to_core(0, e).start()
    for e in (3, 2):
        to_core(0, e).wait_recv()
    spread_half(0, zl)
    gather(0, 1).wait_recv()
    to_core(0, 1).start()
    for k in range(2):
        dn_copy(k).start()
    for e in range(2):
        to_core(0, e).wait_recv()
    spread_half(0, 1 - zl)
    mirror().wait_recv()
    for e in range(3):
        gather(1, e).start()
    to_core(1, 3).start()

    @pl.loop(0, chunks)
    def _(j):
        gu_copy(j).wait()
        up_chunk(0, j)

    early = 2
    for j in range(early):
        finish(j)
    for e in (2, 0, 1):
        gather(1, e).wait_recv()
        to_core(1, e).start()
    for e in range(4):
        to_core(1, e).wait_recv()
    for h in range(2):
        spread_half(1, h)
    lag = 5

    @pl.loop(0, chunks)
    def _(j):
        up_chunk(1, j)

        @pl.when(j < mid - early)
        def _():
            finish(early + j)

        @pl.when(j >= lag)
        def _():
            finish(chunks + j - lag)

    mark = lax.broadcasted_iota(jnp.int32, (group, 128), 1)

    def scale_of(g):
        lanes = xg[g, :, :, width : width + 128].reshape(group, 128).astype(jnp.float32)
        return jnp.sum(jnp.where(lax.rem(mark, n) == me, lanes, 0.0), axis=1, keepdims=True)

    scales = [scale_of(g) for g in range(2)]

    def hidden_cols(g, j0, j1):
        return jnp.concatenate(
            [hid[g * chunks + j].reshape(group, cw) for j in range(j0, j1)], axis=1
        )

    def core_send(g, q):
        return remote(cbuf.at[g, q, 1 - c], crec.at[g, q], rc_s.at[g, q], rc_r.at[g, q], core_peer)

    def near_send(g, q, e):
        a, b = near[e]
        return remote(
            rbuf.at[g, q, a * 2 + b], rrec.at[g, q, e], rr_s.at[g, q, e], rr_r.at[g, q, e], near_peers[e]
        )

    def far_send(q):
        cols = pl.ds(q * pw, pw)
        return remote(fbuf.at[q], far_ref.at[:, cols], rf_s.at[q], rf_r.at[q], far_peer)

    def hand_out(g, q, made):
        mixed = (made.astype(jnp.bfloat16).astype(jnp.float32) * scales[g]).astype(jnp.bfloat16)
        mixed = mixed.reshape(8, rows, pw)
        for b in range(8):
            cbuf[g, q, b % 2, b // 2] = mixed[b]
        core_send(g, q).start()

    def first_part(g, q):
        cols = slice(q * pw, (q + 1) * pw)
        dacc[g, :, cols] = jnp.dot(
            hidden_cols(g, 0, mid), wdn[: mid * cw, cols], preferred_element_type=jnp.float32
        )

    def second_part(g, q):
        cols = slice(q * pw, (q + 1) * pw)
        made = dacc[g, :, cols] + jnp.dot(
            hidden_cols(g, mid, chunks), wdn[mid * cw :, cols], preferred_element_type=jnp.float32
        )
        hand_out(g, q, made)

    def over_core(g, q):
        core_send(g, q).wait_recv()
        rbuf[g, q] = (cbuf[g, q, c].astype(jnp.float32) + crec[g, q].astype(jnp.float32)).astype(jnp.bfloat16)
        for e in range(3):
            near_send(g, q, e).start()

    def over_near(g, q):
        total = rbuf[g, q, zl * 2 + y].astype(jnp.float32)
        for e in range(3):
            near_send(g, q, e).wait_recv()
            total = total + rrec[g, q, e].astype(jnp.float32)
        if g == 0:
            oacc[q] = total
            put(q).start()
        else:
            fbuf[q] = total.astype(jnp.bfloat16)
            far_send(q).start()

    def put(q):
        return pltpu.make_async_copy(oacc.at[q], near_ref.at[:, pl.ds(q * pw, pw)], out_sem.at[q])

    for k in range(2):
        dn_copy(k).wait()
    for s in range(mid):
        hidden_recv(s).wait_recv()
    late = [2 * chunks - lag + i for i in range(lag)]
    spare = list(range(mid, chunks))
    for q in range(pieces):
        first_part(0, q)
        if q % 2 == 1 and late:
            finish(late.pop(0))
            if spare:
                finish(spare.pop(0))
    while late:
        if spare:
            finish(spare.pop(0))
        finish(late.pop(0))
    while spare:
        finish(spare.pop(0))
    for s in range(chunks, chunks + mid):
        hidden_recv(s).wait_recv()
    for q in range(pieces):
        first_part(1, q)
    for s in range(chunks + mid, 2 * chunks):
        hidden_recv(s).wait_recv()
    behind = 4
    for q in range(pieces):
        second_part(1, q)
        if q >= behind:
            over_core(1, q - behind)
    for s in range(mid, chunks):
        hidden_recv(s).wait_recv()
    for q in range(pieces):
        second_part(0, q)
        if pieces - behind + q < pieces:
            over_core(1, pieces - behind + q)
        if q >= behind:
            over_core(0, q - behind)
    for q in range(pieces - behind, pieces):
        over_core(0, q)
    for q in range(pieces):
        over_near(1, q)
    for q in range(pieces):
        over_near(0, q)
    for q in range(pieces):
        far_send(q).wait_recv()

    mirror().wait_send()
    for g in range(2):
        for e in range(3):
            gather(g, e).wait_send()
        for e in range(4):
            to_core(g, e).wait_send()
        for q in range(pieces):
            core_send(g, q).wait_send()
            for e in range(3):
                near_send(g, q, e).wait_send()
    for s in range(2 * chunks):
        partial_send(s).wait_send()
        hidden_send(s).wait_send()
    for q in range(pieces):
        far_send(q).wait_send()
        put(q).wait()


def fused_on_device(tokens, gate_up, w_down, routes, gates):
    _, rows, width = tokens.shape
    hidden_units = w_down.shape[1]
    chunks, pieces = hidden_units // 256, width // 512
    pw, group, half = width // pieces, 8 * rows, 4 * rows
    bf16, dma = jnp.bfloat16, pltpu.SemaphoreType.DMA
    anywhere = pl.BlockSpec(memory_space=pl.ANY)
    near_sum, far_sum = pl.pallas_call(
        functools.partial(fused_kernel, chunks, pieces),
        out_shape=[
            jax.ShapeDtypeStruct((rows, width), jnp.float32),
            jax.ShapeDtypeStruct((rows, width), bf16),
        ],
        in_specs=[anywhere] * 5,
        out_specs=[anywhere] * 2,
        scratch_shapes=[
            pltpu.VMEM((2, 8, rows, width + 128), bf16),
            pltpu.VMEM((chunks, 2 * width, 256), bf16),
            pltpu.VMEM((hidden_units, width), bf16),
            pltpu.VMEM((2, 2, group, 2 * width), bf16),
            pltpu.VMEM((2 * chunks, 2, 2 * half, 256), bf16),
            pltpu.VMEM((2 * chunks, 2 * half, 256), bf16),
            pltpu.VMEM((2 * chunks, 2, half, 256), bf16),
            pltpu.VMEM((2, group, width), jnp.float32),
            pltpu.VMEM((2, pieces, 2, 4, rows, pw), bf16),
            pltpu.VMEM((2, pieces, 4, rows, pw), bf16),
            pltpu.VMEM((2, pieces, 4, rows, pw), bf16),
            pltpu.VMEM((2, pieces, 3, rows, pw), bf16),
            pltpu.VMEM((pieces, rows, pw), jnp.float32),
            pltpu.VMEM((pieces, rows, pw), bf16),
            pltpu.VMEM(routes.shape[1:], routes.dtype),
            pltpu.VMEM(gates.shape[1:], gates.dtype),
            dma((3,)), dma((pieces,)), dma((chunks,)), dma((2,)),
            dma((2, 3)), dma((2, 3)), dma(()), dma(()), dma((2, 4)), dma((2, 4)),
            dma((2 * chunks,)), dma((2 * chunks,)), dma((2 * chunks,)), dma((2 * chunks,)),
            dma((2, pieces)), dma((2, pieces)), dma((2, pieces, 3)), dma((2, pieces, 3)),
            dma((pieces,)), dma((pieces,)),
        ],
        compiler_params=pltpu.CompilerParams(
            collective_id=0, has_side_effects=True, vmem_limit_bytes=67043328
        ),
    )(tokens[0], gate_up[0], w_down[0], routes[0], gates[0])
    return (near_sum + far_sum.astype(jnp.float32)).astype(bf16)[None]


def fits(mesh):
    return mesh.shape["rep"] == 2 and mesh.shape["exp"] == 16


def solution(mesh):
    placed = (
        P(None, "exp", "rep"),
        P("exp", "rep", None, None),
        P("exp", None, "rep"),
        P(None, "exp", None),
        P(None, "exp", None),
    )
    return jax.shard_map(
        fused_on_device if fits(mesh) else on_device, mesh=mesh, in_specs=placed, out_specs=P(None, "exp", "rep"), check_vma=False
    )
```

```python
import functools

import jax
import jax.numpy as jnp
from jax import lax
from jax.experimental import pallas as pl
from jax.experimental.pallas import tpu as pltpu
from jax.sharding import PartitionSpec as P


def silu_glu(summed):
    return (jax.nn.silu(summed[:, 0]) * summed[:, 1]).astype(jnp.bfloat16)


def on_device(tokens, gate_up, w_down, routes, gates):
    steps_all, local_tokens, slab_width = tokens.shape
    top_count = routes.shape[2]
    groups = lax.axis_size("exp")
    experts = gate_up.shape[0] * groups
    capacity = max(2, 2 * local_tokens * top_count // experts)
    hidden_units = w_down.shape[1]
    row_count = groups * capacity
    weights_in = gate_up[0].reshape(slab_width, 2 * hidden_units)
    weights_out = w_down[0]
    labels = jnp.arange(experts * capacity, dtype=jnp.int32)
    expert_range = jnp.arange(experts, dtype=jnp.int32)
    expert_ids = routes[0].reshape(-1)
    onehot = (expert_ids[:, None] == expert_range[None, :]).astype(jnp.int32)
    before = jnp.cumsum(onehot, axis=0) - onehot
    slot_rank = jnp.sum(before * onehot, axis=1)
    target_row = expert_ids * capacity + slot_rank
    target_grid = target_row.reshape(local_tokens, top_count)
    placing = jnp.sum(
        (labels[:, None, None] == target_grid[None, :, :]).astype(jnp.int32), axis=2
    ).astype(jnp.bfloat16)
    outgoing = jnp.dot(placing, tokens[0], preferred_element_type=jnp.float32).astype(jnp.bfloat16)
    outgoing = outgoing.reshape(experts, capacity, slab_width)
    arrived = lax.all_to_all(outgoing, "exp", split_axis=0, concat_axis=0, tiled=True)
    partial_value = jnp.dot(
        arrived.reshape(row_count, slab_width), weights_in, preferred_element_type=jnp.float32
    )
    partial_value = partial_value.reshape(row_count, 2, hidden_units)
    shares = lax.psum_scatter(
        partial_value.astype(jnp.bfloat16), "rep", scatter_dimension=0, tiled=True
    ).astype(jnp.float32)
    hidden = silu_glu(shares)
    produced = jnp.dot(
        lax.all_gather(hidden, "rep", axis=0, tiled=True),
        weights_out,
        preferred_element_type=jnp.float32,
    )
    expert_out = produced.astype(jnp.bfloat16).reshape(groups, capacity, slab_width)
    returned = lax.all_to_all(expert_out, "exp", split_axis=0, concat_axis=0, tiled=True).reshape(
        experts * capacity, slab_width
    )
    picked = returned[target_row].reshape(local_tokens, top_count, slab_width).astype(jnp.float32)
    mixed_out = jnp.sum(gates[0][:, :, None] * picked, axis=1).astype(jnp.bfloat16)
    outputs = [mixed_out]
    return jnp.stack(outputs)


def fused_kernel(
    chunks, pieces, tok_ref, gu_ref, dn_ref, routes_ref, gates_ref, near_ref, far_ref,
    xg, wgu, wdn, x2, pbuf, prec, hid, dacc, cbuf, crec, rbuf, rrec, oacc, fbuf,
    picks, shares, in_sem, out_sem, gu_sem, dn_sem, ag_s, ag_r, mi_s, mi_r, dc_s, dc_r,
    ps_s, ps_r, hs_s, hs_r, rc_s, rc_r, rr_s, rr_r, rf_s, rf_r,
):
    rep = lax.axis_index("rep")
    me = lax.axis_index("exp")
    c, y, zl, pair = lax.rem(me, 2), lax.rem(me // 2, 2), lax.rem(me // 4, 2), me // 8
    rows, width = tok_ref.shape
    hidden_units = dn_ref.shape[0]
    n = 16
    cw, pw = hidden_units // chunks, width // pieces
    group, half = 8 * rows, 4 * rows
    other = 1 - rep
    at = zl * 4 + y * 2 + c
    base = pair * 8
    x_peer = (other, me)
    core_peer = (rep, base + zl * 4 + y * 2 + 1 - c)
    far_peer = (rep, (1 - pair) * 8 + at)
    near = [
        (1 - zl, y),
        (1 - zl, 1 - y),
        (zl, 1 - y),
    ]
    near_peers = [(rep, base + a * 4 + b * 2 + c) for a, b in near]

    def remote(src, dst, send, recv, to):
        return pltpu.make_async_remote_copy(
            src_ref=src, dst_ref=dst, send_sem=send, recv_sem=recv,
            device_id=to, device_id_type=pl.DeviceIdType.MESH,
        )

    barrier = pltpu.get_barrier_semaphore()
    peers = [x_peer, core_peer, far_peer] + near_peers
    for peer in peers:
        pl.semaphore_signal(barrier, inc=1, device_id=peer, device_id_type=pl.DeviceIdType.MESH)

    gu_rows = gu_ref.reshape(2 * width, hidden_units)

    def gu_copy(j):
        return pltpu.make_async_copy(
            gu_rows.at[:, pl.ds(pl.multiple_of(j * cw, 128), cw)], wgu.at[j], gu_sem.at[j]
        )

    mid = chunks // 2

    def dn_copy(k):
        part = pl.ds(k * mid * cw, mid * cw)
        return pltpu.make_async_copy(dn_ref.at[part], wdn.at[part], dn_sem.at[k])

    own = [
        pltpu.make_async_copy(routes_ref, picks, in_sem.at[0]),
        pltpu.make_async_copy(gates_ref, shares, in_sem.at[1]),
        pltpu.make_async_copy(tok_ref, xg.at[0, at, :, pl.ds(0, width)], in_sem.at[2]),
    ]
    for copy in own:
        copy.start()
    for j in range(chunks):
        gu_copy(j).start()
    own[0].wait()
    own[1].wait()
    lane = lax.broadcasted_iota(jnp.int32, (rows, 128), 1)
    weight = jnp.zeros((rows, 128), jnp.float32)
    for k in range(picks.shape[1]):
        hit = picks[:, k : k + 1] == lax.rem(lane, n)
        weight = weight + jnp.where(hit, shares[:, k : k + 1], 0.0)
    high = weight.astype(jnp.bfloat16).astype(jnp.float32)
    packed = jnp.where(lane < n, high, jnp.where(lane < 2 * n, weight - high, 0.0))
    xg[0, at, :, width : width + 128] = packed.astype(jnp.bfloat16)
    own[2].wait()
    pl.semaphore_wait(barrier, len(peers))

    def gather(g, e):
        slot = xg.at[g, at]
        return remote(slot, slot, ag_s.at[g, e], ag_r.at[g, e], near_peers[e])

    def mirror():
        return remote(xg.at[0, at], xg.at[1, at], mi_s, mi_r, far_peer)

    def to_core(g, e):
        a, b = (near + [(zl, y)])[e]
        slot = xg.at[g, a * 4 + b * 2 + c]
        return remote(slot, slot, dc_s.at[g, e], dc_r.at[g, e], core_peer)

    def spread_half(g, h):
        row_at = lax.broadcasted_iota(jnp.int32, (128, 512), 0)
        col_at = lax.broadcasted_iota(jnp.int32, (128, 512), 1)
        target = jnp.where(col_at < 256, 2 * row_at, 256 + 2 * row_at + 1)
        spread = jnp.where(col_at == target, 1.0, 0.0).astype(jnp.bfloat16)
        batch = 14

        @pl.loop(0, width // (128 * batch))
        def _(t):
            parts = [
                xg[g, pl.ds(h * 4, 4), :, pl.ds(pl.multiple_of((t * batch + i) * 128, 128), 128)].reshape(half, 128)
                for i in range(batch)
            ]
            both = jnp.dot(
                jnp.concatenate(parts, axis=0), spread, preferred_element_type=jnp.float32
            ).astype(jnp.bfloat16)
            for i in range(batch):
                cols = pl.ds(pl.multiple_of((t * batch + i) * 256, 256), 256)
                x2[g, h, :half, cols] = both[i * half : (i + 1) * half, :256]
                x2[g, h, half:, cols] = both[i * half : (i + 1) * half, 256:]

    def partial_send(s):
        return remote(pbuf.at[s, other], prec.at[s], ps_s.at[s], ps_r.at[s], x_peer)

    def hidden_send(s):
        return remote(hid.at[s, rep], hid.at[s, rep], hs_s.at[s], hs_r.at[s], x_peer)

    def hidden_recv(s):
        return remote(hid.at[s, other], hid.at[s, other], hs_s.at[s], hs_r.at[s], x_peer)

    def finish(s):
        partial_send(s).wait_recv()
        total = pbuf[s, rep].astype(jnp.float32) + prec[s].astype(jnp.float32)
        hid[s, rep] = (jax.nn.silu(total[:half]) * total[half:]).astype(jnp.bfloat16)
        hidden_send(s).start()

    def up_chunk(g, j):
        acc = jnp.dot(x2[g].reshape(2 * group, 2 * width), wgu[j], preferred_element_type=jnp.float32)
        pbuf[g * chunks + j] = acc.astype(jnp.bfloat16).reshape(2, 2 * half, cw)
        partial_send(g * chunks + j).start()

    for e in (1, 2, 0):
        gather(0, e).start()
    to_core(0, 3).start()
    mirror().start()
    for e in (2, 0):
        gather(0, e).wait_recv()
        to_core(0, e).start()
    for e in (3, 2):
        to_core(0, e).wait_recv()
    spread_half(0, zl)
    gather(0, 1).wait_recv()
    to_core(0, 1).start()
    for k in range(2):
        dn_copy(k).start()
    for e in range(2):
        to_core(0, e).wait_recv()
    spread_half(0, 1 - zl)
    mirror().wait_recv()
    for e in (1, 2, 0):
        gather(1, e).start()
    to_core(1, 3).start()

    @pl.loop(0, chunks)
    def _(j):
        gu_copy(j).wait()
        up_chunk(0, j)

    early = 2
    for j in range(early):
        finish(j)
    for e in (2, 0, 1):
        gather(1, e).wait_recv()
        to_core(1, e).start()
    for e in range(4):
        to_core(1, e).wait_recv()
    for h in range(2):
        spread_half(1, h)
    lag = 5

    @pl.loop(0, chunks)
    def _(j):
        up_chunk(1, j)

        @pl.when(j < mid - early)
        def _():
            finish(early + j)

        @pl.when(j >= lag)
        def _():
            finish(chunks + j - lag)

    mark = lax.broadcasted_iota(jnp.int32, (group, 128), 1)

    def scale_of(g):
        lanes = xg[g, :, :, width : width + 128].reshape(group, 128).astype(jnp.float32)
        return jnp.sum(jnp.where(lax.rem(mark, n) == me, lanes, 0.0), axis=1, keepdims=True)

    scales = [scale_of(g) for g in range(2)]

    def hidden_cols(g, j0, j1):
        return jnp.concatenate(
            [hid[g * chunks + j].reshape(group, cw) for j in range(j0, j1)], axis=1
        )

    def core_send(g, q):
        return remote(cbuf.at[g, q, 1 - c], crec.at[g, q], rc_s.at[g, q], rc_r.at[g, q], core_peer)

    def near_send(g, q, e):
        a, b = near[e]
        return remote(
            rbuf.at[g, q, a * 2 + b], rrec.at[g, q, e], rr_s.at[g, q, e], rr_r.at[g, q, e], near_peers[e]
        )

    def far_send(q):
        cols = pl.ds(q * pw, pw)
        return remote(fbuf.at[q], far_ref.at[:, cols], rf_s.at[q], rf_r.at[q], far_peer)

    def hand_out(g, q, made):
        mixed = (made.astype(jnp.bfloat16).astype(jnp.float32) * scales[g]).astype(jnp.bfloat16)
        mixed = mixed.reshape(8, rows, pw)
        for b in range(8):
            cbuf[g, q, b % 2, b // 2] = mixed[b]
        core_send(g, q).start()

    def first_part(g, q):
        cols = slice(q * pw, (q + 1) * pw)
        dacc[g, :, cols] = jnp.dot(
            hidden_cols(g, 0, mid), wdn[: mid * cw, cols], preferred_element_type=jnp.float32
        )

    def second_part(g, q):
        cols = slice(q * pw, (q + 1) * pw)
        made = dacc[g, :, cols] + jnp.dot(
            hidden_cols(g, mid, chunks), wdn[mid * cw :, cols], preferred_element_type=jnp.float32
        )
        hand_out(g, q, made)

    def over_core(g, q):
        core_send(g, q).wait_recv()
        rbuf[g, q] = (cbuf[g, q, c].astype(jnp.float32) + crec[g, q].astype(jnp.float32)).astype(jnp.bfloat16)
        for e in (1, 2, 0):
            near_send(g, q, e).start()

    def over_near(g, q):
        total = rbuf[g, q, zl * 2 + y].astype(jnp.float32)
        for e in range(3):
            near_send(g, q, e).wait_recv()
            total = total + rrec[g, q, e].astype(jnp.float32)
        if g == 0:
            oacc[q] = total
            put(q).start()
        else:
            fbuf[q] = total.astype(jnp.bfloat16)
            far_send(q).start()

    def put(q):
        return pltpu.make_async_copy(oacc.at[q], near_ref.at[:, pl.ds(q * pw, pw)], out_sem.at[q])

    for k in range(2):
        dn_copy(k).wait()
    for s in range(mid):
        hidden_recv(s).wait_recv()
    late = [2 * chunks - lag + i for i in range(lag)]
    spare = list(range(mid, chunks))
    for q in range(pieces):
        first_part(0, q)
        if q % 2 == 1 and late:
            finish(late.pop(0))
            if spare:
                finish(spare.pop(0))
    while late:
        if spare:
            finish(spare.pop(0))
        finish(late.pop(0))
    while spare:
        finish(spare.pop(0))
    for s in range(chunks, chunks + mid):
        hidden_recv(s).wait_recv()
    for q in range(pieces):
        first_part(1, q)
    for s in range(chunks + mid, 2 * chunks):
        hidden_recv(s).wait_recv()
    behind = 4
    for q in range(pieces):
        second_part(1, q)
        if q >= behind:
            over_core(1, q - behind)
    for s in range(mid, chunks):
        hidden_recv(s).wait_recv()
    for q in range(pieces):
        second_part(0, q)
        if pieces - behind + q < pieces:
            over_core(1, pieces - behind + q)
        if q >= behind:
            over_core(0, q - behind)
    for q in range(pieces - behind, pieces):
        over_core(0, q)
    for q in range(pieces):
        over_near(1, q)
    for q in range(pieces):
        over_near(0, q)
    for q in range(pieces):
        far_send(q).wait_recv()

    mirror().wait_send()
    for g in range(2):
        for e in range(3):
            gather(g, e).wait_send()
        for e in range(4):
            to_core(g, e).wait_send()
        for q in range(pieces):
            core_send(g, q).wait_send()
            for e in range(3):
                near_send(g, q, e).wait_send()
    for s in range(2 * chunks):
        partial_send(s).wait_send()
        hidden_send(s).wait_send()
    for q in range(pieces):
        far_send(q).wait_send()
        put(q).wait()


def fused_on_device(tokens, gate_up, w_down, routes, gates):
    _, rows, width = tokens.shape
    hidden_units = w_down.shape[1]
    chunks, pieces = hidden_units // 256, width // 512
    pw, group, half = width // pieces, 8 * rows, 4 * rows
    bf16, dma = jnp.bfloat16, pltpu.SemaphoreType.DMA
    anywhere = pl.BlockSpec(memory_space=pl.ANY)
    near_sum, far_sum = pl.pallas_call(
        functools.partial(fused_kernel, chunks, pieces),
        out_shape=[
            jax.ShapeDtypeStruct((rows, width), jnp.float32),
            jax.ShapeDtypeStruct((rows, width), bf16),
        ],
        in_specs=[anywhere] * 5,
        out_specs=[anywhere] * 2,
        scratch_shapes=[
            pltpu.VMEM((2, 8, rows, width + 128), bf16),
            pltpu.VMEM((chunks, 2 * width, 256), bf16),
            pltpu.VMEM((hidden_units, width), bf16),
            pltpu.VMEM((2, 2, group, 2 * width), bf16),
            pltpu.VMEM((2 * chunks, 2, 2 * half, 256), bf16),
            pltpu.VMEM((2 * chunks, 2 * half, 256), bf16),
            pltpu.VMEM((2 * chunks, 2, half, 256), bf16),
            pltpu.VMEM((2, group, width), jnp.float32),
            pltpu.VMEM((2, pieces, 2, 4, rows, pw), bf16),
            pltpu.VMEM((2, pieces, 4, rows, pw), bf16),
            pltpu.VMEM((2, pieces, 4, rows, pw), bf16),
            pltpu.VMEM((2, pieces, 3, rows, pw), bf16),
            pltpu.VMEM((pieces, rows, pw), jnp.float32),
            pltpu.VMEM((pieces, rows, pw), bf16),
            pltpu.VMEM(routes.shape[1:], routes.dtype),
            pltpu.VMEM(gates.shape[1:], gates.dtype),
            dma((3,)), dma((pieces,)), dma((chunks,)), dma((2,)),
            dma((2, 3)), dma((2, 3)), dma(()), dma(()), dma((2, 4)), dma((2, 4)),
            dma((2 * chunks,)), dma((2 * chunks,)), dma((2 * chunks,)), dma((2 * chunks,)),
            dma((2, pieces)), dma((2, pieces)), dma((2, pieces, 3)), dma((2, pieces, 3)),
            dma((pieces,)), dma((pieces,)),
        ],
        compiler_params=pltpu.CompilerParams(
            collective_id=0, has_side_effects=True, vmem_limit_bytes=67043328
        ),
    )(tokens[0], gate_up[0], w_down[0], routes[0], gates[0])
    return (near_sum + far_sum.astype(jnp.float32)).astype(bf16)[None]


def fits(mesh):
    return mesh.shape["rep"] == 2 and mesh.shape["exp"] == 16


def solution(mesh):
    placed = (
        P(None, "exp", "rep"),
        P("exp", "rep", None, None),
        P("exp", None, "rep"),
        P(None, "exp", None),
        P(None, "exp", None),
    )
    return jax.shard_map(
        fused_on_device if fits(mesh) else on_device, mesh=mesh, in_specs=placed, out_specs=P(None, "exp", "rep"), check_vma=False
    )
```
